256 devices in a mesh: group: 4 (over x), dev: 64 (over y, z, core).
Axes of the slice: x: 4, y: 4, z: 8, core: 2. Of those that a mesh axis runs over, the one named last changes fastest.
Arguments:
- species: float32 [6, 512, 32768], P(None, ('group', 'dev')), may hold values from 0.5 to 2
- potential: float32 [512, 32768], P(('group', 'dev')), may hold values from -4 to 4
- pore: int32 [512, 32768], P(('group', 'dev')), may hold values 0 or 1
- openness: float32 [512, 32768], P(('group', 'dev')), may hold values from 0.3 to 1
- neighbours: int32 [512, 6], P(('group', 'dev')), may hold values from 0 to 1, as said below
- diffusivity: float32 [6], replicated, may hold values from 0.02 to 0.12
- rate_const: float32 [512], P(('group', 'dev')), may hold values from 0.1 to 1
- opened: int32 [512], P(('group', 'dev')), may hold values 0 or 1
- partner: int32 [256], P(('group', 'dev')), may hold values from 0 to 255, as said below
- give_slot: int32 [256], P(('group', 'dev')), may hold values from 0 to 1
Outputs:
- new_species: float32 [6, 512, 32768], P(None, ('group', 'dev'))
- new_potential: float32 [512, 32768], P(('group', 'dev'))
The draws below stay inside these ranges and needn't reach their ends.
Inputs may be any that keep to these rules, and one draw needn't show every extreme that they name: `neighbours`: entry k of brick b names a slot of the device given in the reference program for direction k; the lists are consistent: if brick c is the neighbour of b in direction +x, +y or +z, then b is the neighbour of c in the opposite direction. partner[partner[q]] = q for every device q; a partner other than q differs from q in exactly one bit of the device index; over all devices at most two distinct bits occur, at most one of them below 64.
All inputs are finite; a program needn't handle non-finite values. No bound on the sum of `pore` or of `opened` on one device may be relied on, other than what follows from the above.
Results may differ from the reference program's by a relative error of at most 0.00002.
Values sent between devices are 32-bit elements; how exact they have to be, the bound alone decides.
A program may use at most 128 MiB of HBM per device.

```python
import math
import jax
import jax.numpy as jnp

SIDE = 32
BRICKS = 2
IONS = 6
SWEEPS = 8
CELLS = 32768
STRIDE = 16
TOTAL_BRICKS = 512
N_GROUP = 4
N_DEV = 64


def draw_neighbours(key, part):
    total = N_GROUP * N_DEV
    device = jnp.arange(total, dtype=jnp.int32)
    group_index = device // N_DEV
    dev_index = device % N_DEV
    stride = N_DEV // 4
    behind = [group_index * N_DEV + (dev_index - 1) % N_DEV, group_index * N_DEV + (dev_index - stride) % N_DEV, (group_index - 1) % N_GROUP * N_DEV + dev_index]
    columns = []
    for axis_number in range(3):
        keys = jax.random.split(jax.random.fold_in(key, axis_number + 11), total)
        orders = jax.vmap(lambda single: jax.random.permutation(single, BRICKS))(keys).astype(jnp.int32)
        inverse = jnp.argsort(orders, axis=1, stable=True).astype(jnp.int32)
        columns.append(orders.reshape(-1))
        columns.append(inverse[behind[axis_number]].reshape(-1))
    return jnp.stack(columns, axis=1).astype(jnp.int32)


def draw_partner(key, part):
    total = N_GROUP * N_DEV
    dev_bits = N_DEV.bit_length() - 1
    group_bits = N_GROUP.bit_length() - 1
    first_key, second_key, third_key = jax.random.split(jax.random.fold_in(key, 7), 3)
    inner_bit = jax.random.randint(first_key, (), 0, dev_bits)
    outer_bit = dev_bits + jax.random.randint(second_key, (), 0, group_bits)
    device = jnp.arange(total, dtype=jnp.int32)
    inner_mask = jnp.left_shift(jnp.int32(1), inner_bit.astype(jnp.int32))
    outer_mask = jnp.left_shift(jnp.int32(1), outer_bit.astype(jnp.int32))
    corner = jnp.bitwise_and(device, jnp.bitwise_not(jnp.bitwise_or(inner_mask, outer_mask)))
    modes = jax.random.randint(third_key, (total,), 0, 3)
    mode = modes[corner]
    paired = jnp.where(mode == 1, jnp.bitwise_xor(device, inner_mask), jnp.where(mode == 2, jnp.bitwise_xor(device, outer_mask), device))
    return paired.astype(jnp.int32)


def set_ends(result, own_key, least, high):
    place = [jax.random.randint(jax.random.fold_in(own_key, axis), (), 0, length) for axis, length in enumerate(result.shape)]
    longest = result.shape.index(max(result.shape))
    neighbour = place[:longest] + [(place[longest] + 1) % result.shape[longest]] + place[longest + 1:]
    return result.at[tuple(place)].set(least).at[tuple(neighbour)].set(high)


def block_scale(own_key, extent, cuts, least, largest):
    level = 1.0
    for dim, parts in cuts:
        draws = jax.random.uniform(jax.random.fold_in(jax.random.fold_in(own_key, 6), dim), (parts,), jnp.float32, least / len(cuts), largest / len(cuts))
        level = level * jnp.repeat(jnp.exp(draws), extent[dim] // parts).reshape((-1,) + (1,) * (len(extent) - 1 - dim))
    return level


def normal_values(rng, extent, spread, most, cuts=(), held_as=jnp.bfloat16):
    values = jax.random.normal(rng, extent, jnp.float32) * spread
    if len(cuts) > 0:
        values = block_scale(rng, extent, cuts, -0.22, 0.18) * values
    return jnp.clip(values, min=-most, max=most).astype(held_as)


def setup_inputs(seed: int = 0) -> dict:
    streams_of = jax.random.split(jax.random.key(seed), 11)
    return {
        "species": jnp.clip(0.5 + 1.5 * jax.random.uniform(streams_of[0], (IONS, TOTAL_BRICKS, CELLS), jnp.float32) ** block_scale(streams_of[0], (IONS, TOTAL_BRICKS, CELLS), ((1, 256),), -0.2, 0.2), 0.5, 2.0),
        "potential": normal_values(streams_of[1], (TOTAL_BRICKS, CELLS), 1.0, 4.0, ((0, 256),), jnp.float32),
        "pore": set_ends((jax.random.randint(streams_of[2], (TOTAL_BRICKS, CELLS), 0, 5) < 3).astype(jnp.int32), jax.random.fold_in(streams_of[2], 1), 0, 1),
        "openness": jnp.clip(0.3 + 0.7 * jax.random.uniform(streams_of[3], (TOTAL_BRICKS, CELLS), jnp.float32) ** block_scale(streams_of[3], (TOTAL_BRICKS, CELLS), ((0, 256),), -0.2, 0.2), 0.3, 1.0),
        "neighbours": draw_neighbours(jax.random.fold_in(streams_of[10], 71), 0),
        "diffusivity": jnp.clip(jnp.exp(jax.random.uniform(streams_of[5], (IONS,), jnp.float32, math.log(0.02), math.log(0.12))), 0.02, 0.12),
        "rate_const": jnp.clip(jnp.exp(math.log(1.0) - 2.3025851 * jax.random.uniform(streams_of[6], (TOTAL_BRICKS,), jnp.float32) ** block_scale(streams_of[6], (TOTAL_BRICKS,), ((0, 256),), -0.2, 0.2)), 0.1, 1.0),
        "opened": set_ends((jax.random.randint(streams_of[7], (TOTAL_BRICKS,), 0, 2) < 1).astype(jnp.int32), jax.random.fold_in(streams_of[7], 1), 0, 1),
        "partner": draw_partner(jax.random.fold_in(streams_of[10], 71), 0),
        "give_slot": set_ends(jax.random.randint(streams_of[9], (N_GROUP * N_DEV,), 0, BRICKS), jax.random.fold_in(streams_of[9], 1), 0, BRICKS - 1).astype(jnp.int32),
    }


charge_scale = 0.5
screening = 0.5
solubility = 2.0
valences = (2.0, -1.0, 1.0, -1.0, 1.0, 2.0)
reaction_signs = (1.0, 1.0, -1.0, 0.0, 0.0, 0.0)


def face_list(field):
    brick_side = field.shape[-2]
    cube_view = field.reshape(field.shape[:-1] + (brick_side, brick_side))
    flat_shape = field.shape[:-2] + (brick_side * brick_side,)
    return (field[..., 0, :], field[..., brick_side - 1, :],
            cube_view[..., :, 0, :].reshape(flat_shape), cube_view[..., :, brick_side - 1, :].reshape(flat_shape),
            cube_view[..., 0].reshape(flat_shape), cube_view[..., brick_side - 1].reshape(flat_shape))


def beside_values(field, halo_list):
    brick_side = field.shape[-2]
    plane_shape = field.shape[:-2] + (brick_side, brick_side)
    cube_shape = field.shape[:-2] + (brick_side, brick_side, brick_side)
    east_side = jnp.concatenate([field[..., 1:, :], halo_list[0][..., None, :]], axis=-2)
    west_side = jnp.concatenate([halo_list[1][..., None, :], field[..., :-1, :]], axis=-2)
    north_side = jnp.concatenate([field[..., brick_side:], halo_list[2].reshape(plane_shape)], axis=-1)
    south_side = jnp.concatenate([halo_list[3].reshape(plane_shape), field[..., :-brick_side]], axis=-1)
    depth_index = jnp.arange(brick_side * brick_side, dtype=jnp.int32) % brick_side
    upper_rim = jnp.broadcast_to(halo_list[4].reshape(plane_shape)[..., None], cube_shape).reshape(field.shape)
    lower_rim = jnp.broadcast_to(halo_list[5].reshape(plane_shape)[..., None], cube_shape).reshape(field.shape)
    upper_side = jnp.where(depth_index == brick_side - 1, upper_rim,
                           jnp.concatenate([field[..., 1:], field[..., :1]], axis=-1))
    lower_side = jnp.where(depth_index == 0, lower_rim,
                           jnp.concatenate([field[..., -1:], field[..., :-1]], axis=-1))
    return (east_side, west_side, north_side, south_side, upper_side, lower_side)


def relax(nearby, density):
    total = nearby[0] + nearby[1] + nearby[2] + nearby[3] + nearby[4] + nearby[5] + density
    return total / (6.0 + screening)


def local_update(species, swept, wetted, pore_float, halo_species, halo_swept, halo_wetted, diffusivity, reactivity):
    near_species = beside_values(species, halo_species)
    near_swept = beside_values(swept, halo_swept)
    near_wetted = beside_values(wetted, halo_wetted)
    half_charge = 0.5 * jnp.asarray(valences, jnp.float32)[:, None, None, None]
    outflow = jnp.zeros_like(species)
    for direction in range(6):
        conductance = wetted * near_wetted[direction]
        outflow = outflow + conductance * ((species - near_species[direction])
                                           + half_charge * (species + near_species[direction]) * (swept - near_swept[direction]))
    reaction = reactivity[:, None, None] * pore_float * (species[2] - species[0] * species[1] / solubility)
    signs = jnp.asarray(reaction_signs, jnp.float32)[:, None, None, None]
    return species - diffusivity[:, None, None, None] * outflow + signs * reaction


def global_slots(neighbours):
    slot_index = jnp.arange(TOTAL_BRICKS, dtype=jnp.int32)
    device = slot_index // BRICKS
    group_index = device // N_DEV
    dev_index = device % N_DEV
    owners = [group_index * N_DEV + (dev_index + 1) % N_DEV,
              group_index * N_DEV + (dev_index - 1) % N_DEV,
              group_index * N_DEV + (dev_index + STRIDE) % N_DEV,
              group_index * N_DEV + (dev_index - STRIDE) % N_DEV,
              ((group_index + 1) % N_GROUP) * N_DEV + dev_index,
              ((group_index - 1) % N_GROUP) * N_DEV + dev_index]
    owner_table = jnp.stack(owners, axis=1).astype(jnp.int32)
    return owner_table * BRICKS + neighbours


def gather_halos(field, table):
    faces = face_list(field)
    return tuple(jnp.take(faces[direction], table[:, direction], axis=-2) for direction in range(6))


def reference(species, potential, pore, openness, neighbours, diffusivity, rate_const, opened, partner, give_slot):
    cell_shape = (TOTAL_BRICKS, SIDE, SIDE * SIDE)
    table = global_slots(neighbours)
    species_cube = species.reshape((IONS,) + cell_shape)
    pore_float = pore.astype(jnp.float32).reshape(cell_shape)
    wetted = pore_float * openness.reshape(cell_shape)
    charges = jnp.asarray(valences, jnp.float32)[:, None, None, None]
    density = charge_scale * wetted * jnp.sum(charges * species_cube, axis=0)
    swept = potential.reshape(cell_shape)
    for sweep_index in range(SWEEPS):
        swept = relax(beside_values(swept, gather_halos(swept, table)), density)
    reactivity = rate_const * opened.astype(jnp.float32)
    updated = local_update(species_cube, swept, wetted, pore_float,
                           gather_halos(species_cube, table), gather_halos(swept, table),
                           gather_halos(wetted, table), diffusivity, reactivity)
    device = jnp.arange(N_GROUP * N_DEV, dtype=jnp.int32)
    target = device * BRICKS + give_slot
    source = partner * BRICKS + give_slot[partner]
    anchor = jnp.arange(TOTAL_BRICKS, dtype=jnp.int32).at[target].set(source)
    new_species = updated[:, anchor].reshape(IONS, TOTAL_BRICKS, SIDE * SIDE * SIDE)
    new_potential = swept[anchor].reshape(TOTAL_BRICKS, SIDE * SIDE * SIDE)
    return new_species, new_potential
```

```python
from functools import partial

import jax
import jax.numpy as jnp
from jax import lax
from jax.experimental import pallas as pl
from jax.experimental.pallas import tpu as pltpu
from jax.sharding import PartitionSpec as P

MESH = pl.DeviceIdType.MESH

SIDE = 32
SWEEPS = 8
ROWS = 512
PAD = 16
N_GROUP = 4
N_DEV = 64

charge_scale = 0.5
screening = 0.5
solubility = 2.0
valences = (2.0, -1.0, 1.0, -1.0, 1.0, 2.0)
reaction_signs = (1.0, 1.0, -1.0, 0.0, 0.0, 0.0)
IONS = len(valences)
FIELDS = IONS + 1
INV = 1.0 / (6.0 + screening)


def iotas():
    row = lax.broadcasted_iota(jnp.int32, (8, 128), 0)
    lane = lax.broadcasted_iota(jnp.int32, (8, 128), 1)
    return row, lane


def lroll(v, shift):
    if isinstance(shift, int):
        shift %= 128
        return v if shift == 0 else pltpu.roll(v, shift, 1)
    return pltpu.roll(v, shift, 1)


def sroll(v, shift):
    shift %= 8
    return v if shift == 0 else pltpu.roll(v, shift, 0)


def flipped(group, dev, bit):
    q = group * N_DEV + dev
    mask = 2**bit
    other = q + (1 - 2 * ((q // mask) % 2)) * mask
    return {"group": other // N_DEV, "dev": other % N_DEV}


def plane_rows(x):
    return pl.multiple_of(x * 16, 16)


def pack_start():
    zero = jnp.zeros((8, 128), jnp.float32)
    return (zero,) * 8


def pack_planes(acc, xi, planes, row, lane):
    acc = list(acc)
    for j in range(2):
        low = high = None
        for i in range(4):
            a, b = planes[4 * j + i]
            first, last = sroll(a, 2 * i), sroll(b, 2 * i - 6)
            low = first if low is None else jnp.where(row // 2 == i, first, low)
            high = last if high is None else jnp.where(row // 2 == i, last, high)
        here = lane // 32 == xi
        acc[j] = jnp.where(here, lroll(low, 32 * xi), acc[j])
        acc[2 + j] = jnp.where(here, lroll(high, (32 * xi + 32) % 128), acc[2 + j])
    for i in range(8):
        x = 4 * i + xi
        z0, z1 = lane % 32 == x, lane % 32 == (x + 31) % 32
        for h in range(2):
            turned = lroll(planes[i][h], x)
            acc[4 + h] = jnp.where(z0, turned, acc[4 + h])
            acc[6 + h] = jnp.where(z1, turned, acc[6 + h])
    return tuple(acc)


def pack_end(acc):
    return acc[:6] + (lroll(acc[6], 97), lroll(acc[7], 97))


def around(a, b, x, i, turned, above, below, row, lane):
    north, south = turned
    ra, rb = lroll(a, 96), lroll(b, 96)
    ua, ub = sroll(ra, 6), sroll(rb, 6)
    edge = sroll(north[i // 4], 6 - 2 * (i % 4))
    na = jnp.where(lane < 96, ra, jnp.where(row < 6, ua, ub))
    nb = jnp.where(lane < 96, rb, jnp.where(row < 6, ub, edge))
    qa, qb = lroll(a, 32), lroll(b, 32)
    da, db = sroll(qa, 2), sroll(qb, 2)
    edge = sroll(south[i // 4], -2 * (i % 4))
    sa = jnp.where(lane >= 32, qa, jnp.where(row >= 2, da, edge))
    sb = jnp.where(lane >= 32, qb, jnp.where(row >= 2, db, da))
    top, bottom = lane % 32 == 31, lane % 32 == 0
    up = [jnp.where(top, lroll(above[h], 31 - x), lroll(v, 127)) for h, v in enumerate((a, b))]
    down = [
        jnp.where(bottom, lroll(below[h], (128 - x) % 128), lroll(v, 1)) for h, v in enumerate((a, b))
    ]
    return (na, sa, up[0], down[0]), (nb, sb, up[1], down[1])


def turn_faces(faces, xi):
    north = [lroll(v, (96 + 128 - 32 * xi) % 128) for v in faces[0]]
    south = [lroll(v, (128 - 32 * xi) % 128) for v in faces[1]]
    return north, south


def step_kernel(
    potential,
    pore,
    openness,
    species,
    neighbours,
    diffusivity,
    rate_const,
    opened,
    partner,
    give_slot,
    updated,
    outgoing,
    choice,
    phi,
    conc,
    near,
    dens,
    pore_in,
    open_in,
    packed,
    arrived,
    packed_all,
    arrived_all,
    flag,
    flag_in,
    load_sems,
    send_sems,
    recv_sems,
    send_all_sems,
    recv_all_sems,
    flag_send,
    flag_recv,
):
    row, lane = iotas()
    even = row % 2 == 0
    group, dev = lax.axis_index("group"), lax.axis_index("dev")
    loads = [
        pltpu.make_async_copy(potential, phi.at[0, pl.ds(PAD, ROWS)], load_sems.at[0]),
        pltpu.make_async_copy(pore, pore_in, load_sems.at[1]),
        pltpu.make_async_copy(openness, open_in, load_sems.at[2]),
    ] + [
        pltpu.make_async_copy(species.at[i], conc.at[i, pl.ds(PAD, ROWS)], load_sems.at[3 + i])
        for i in range(IONS)
    ]
    for load in loads:
        load.start()

    targets = [
        {"dev": (dev + N_DEV - 1) % N_DEV},
        {"dev": (dev + 1) % N_DEV},
        {"dev": (dev + N_DEV - 16) % N_DEV},
        {"dev": (dev + 16) % N_DEV},
        {"group": (group + N_GROUP - 1) % N_GROUP},
        {"group": (group + 1) % N_GROUP},
    ]
    flips = [flipped(group, dev, bit) for bit in range(8)]
    barrier = pltpu.get_barrier_semaphore()
    for target in targets + flips:
        pl.semaphore_signal(barrier, inc=1, device_id=target, device_id_type=MESH)

    keep = []
    for k in range(6):
        slots = jnp.where(even, neighbours[0, k], neighbours[1, k])
        keep.append(slots == row % 2)

    def chosen(k, v):
        return jnp.where(keep[k], v, jnp.where(even, sroll(v, 7), sroll(v, 1)))

    def chosen_face(ref, k):
        return [chosen(k, ref[0:8, :]), chosen(k, ref[8:16, :])]

    zeros = jnp.zeros((PAD, 128), jnp.float32)
    for s in range(2):
        phi[s, 0:PAD, :] = zeros
        phi[s, PAD + ROWS : PAD + ROWS + PAD, :] = zeros

    def sends(state):
        slot = state % 2
        sources = [phi.at[slot, pl.ds(PAD, 16)], phi.at[slot, pl.ds(ROWS, 16)]] + [
            packed.at[state, k - 2] for k in range(2, 6)
        ]
        return [
            pltpu.make_async_remote_copy(
                src_ref=sources[k],
                dst_ref=arrived.at[state, k],
                send_sem=send_sems.at[state, k],
                recv_sem=recv_sems.at[state, k],
                device_id=targets[k],
                device_id_type=MESH,
            )
            for k in range(6)
        ]

    def put_faces(ref_of, acc):
        for k in range(4):
            ref = ref_of(k)
            ref[0:8, :] = acc[2 * k]
            ref[8:16, :] = acc[2 * k + 1]

    def pack_field(read):
        def step(xi, acc):
            planes = []
            for i in range(8):
                r = plane_rows(4 * i + xi) + PAD
                planes.append((read(r), read(r + 8)))
            return pack_planes(acc, xi, planes, row, lane)

        return pack_end(lax.fori_loop(0, 4, step, pack_start()))

    loads[0].wait()
    acc = pack_field(lambda r: phi[0, pl.ds(pl.multiple_of(r, 8), 8), :])
    put_faces(lambda k: packed.at[0, k], acc)
    me = group * N_DEV + dev
    flag[0] = jnp.where(
        lane < 8,
        jnp.where(
            jnp.bitwise_xor(partner[0], me) == lax.shift_left(jnp.ones_like(lane), lane % 8), 1.0, 0.0
        ),
        0.0,
    )
    pl.semaphore_wait(barrier, len(targets) + len(flips))
    for copy in sends(0):
        copy.start()

    for load in loads[1:]:
        load.wait()

    def prepare(x, carry):
        for h in range(2):
            r = pl.multiple_of(x * 16 + 8 * h, 8)
            rows, inner = pl.ds(r, 8), pl.ds(pl.multiple_of(r + PAD, 8), 8)
            wet = pore_in[rows, :].astype(jnp.float32) * open_in[rows, :]
            conc[IONS, inner, :] = wet
            total = valences[0] * conc[0, inner, :]
            for i in range(1, IONS):
                total = total + valences[i] * conc[i, inner, :]
            dens[rows, :] = (charge_scale * INV) * wet * total
        return carry

    lax.fori_loop(0, SIDE, prepare, 0)

    def pack_one(f, carry):
        acc = pack_field(lambda r: conc[f, pl.ds(pl.multiple_of(r, 8), 8), :])
        put_faces(lambda k: packed_all.at[k, f], acc)
        return carry

    lax.fori_loop(0, FIELDS, pack_one, 0)
    sources = [conc.at[:, pl.ds(PAD, 16)], conc.at[:, pl.ds(ROWS, 16)]] + [
        packed_all.at[k] for k in range(4)
    ]
    all_sends = [
        pltpu.make_async_remote_copy(
            src_ref=sources[k],
            dst_ref=arrived_all.at[k],
            send_sem=send_all_sems.at[k],
            recv_sem=recv_all_sems.at[k],
            device_id=targets[k],
            device_id_type=MESH,
        )
        for k in range(6)
    ]
    for copy in all_sends:
        copy.start()

    def flag_copy(bit):
        return pltpu.make_async_remote_copy(
            src_ref=flag.at[bit],
            dst_ref=flag_in.at[bit],
            send_sem=flag_send.at[bit],
            recv_sem=flag_recv.at[bit],
            device_id=flips[bit],
            device_id_type=MESH,
        )

    def near_field(f, read, halo):
        faces = [chosen_face(halo(k), k) for k in range(2, 6)]

        def step(xi, carry):
            turned = turn_faces(faces[:2], xi)
            for i in range(8):
                x = 4 * i + xi
                r = plane_rows(x)
                a, b = read(r + PAD), read(r + PAD + 8)
                both = around(a, b, x, i, turned, faces[2], faces[3], row, lane)
                for h in range(2):
                    rows = pl.ds(pl.multiple_of(r + 8 * h, 8), 8)
                    for n in range(4):
                        near[f, n, rows, :] = both[h][n]
            return carry

        lax.fori_loop(0, 4, step, 0)

    def sweep(t, carry):
        old, new = t % 2, (t + 1) % 2
        for bit in range(8):

            @pl.when(t == bit)
            def _(bit=bit):
                flag_copy(bit).start()

        copies = sends(t)
        for k in range(2, 6):
            copies[k].wait_recv()
        faces = [chosen_face(arrived.at[t, k], k) for k in range(2, 6)]

        def read(r):
            return phi[old, pl.ds(pl.multiple_of(r, 8), 8), :]

        def step(xi, acc):
            turned = turn_faces(faces[:2], xi)
            planes = []
            for i in range(8):
                x = 4 * i + xi
                r = plane_rows(x)
                a, b = read(r + PAD), read(r + PAD + 8)
                both = around(a, b, x, i, turned, faces[2], faces[3], row, lane)
                out = []
                for h in range(2):
                    rows = pl.ds(pl.multiple_of(r + 8 * h, 8), 8)
                    total = read(r + 8 * h) + read(r + 8 * h + 2 * PAD)
                    for value in both[h]:
                        total = total + value
                    value = total * INV + dens[rows, :]
                    phi[new, pl.ds(pl.multiple_of(r + 8 * h + PAD, 8), 8), :] = value
                    out.append(value)
                planes.append(tuple(out))
            return pack_planes(acc, xi, planes, row, lane)

        acc = list(pack_end(lax.fori_loop(0, 4, step, pack_start())))
        for k in range(2):
            copies[k].wait_recv()
        for copy in copies:
            copy.wait_send()
        ends = []
        for k, base in ((1, PAD), (0, ROWS)):
            halo = chosen_face(arrived.at[t, k], k)
            pair = []
            for h in range(2):
                value = phi[new, base + 8 * h : base + 8 * h + 8, :] + halo[h] * INV
                phi[new, base + 8 * h : base + 8 * h + 8, :] = value
                pair.append(value)
            ends.append(pair)
        (fa, fb), (la, lb) = ends
        first = (row < 2) & (lane < 32)
        last = (row >= 6) & (lane >= 96)
        acc[0] = jnp.where(first, fa, acc[0])
        acc[2] = jnp.where(first, lroll(sroll(fb, 2), 32), acc[2])
        acc[1] = jnp.where(last, lroll(sroll(la, 6), 96), acc[1])
        acc[3] = jnp.where(last, lb, acc[3])
        for h in range(2):
            acc[4 + h] = jnp.where(lane % 32 == 0, (fa, fb)[h], acc[4 + h])
            acc[4 + h] = jnp.where(lane % 32 == 31, lroll((la, lb)[h], 31), acc[4 + h])
            acc[6 + h] = jnp.where(lane % 32 == 0, lroll((fa, fb)[h], 97), acc[6 + h])
            acc[6 + h] = jnp.where(lane % 32 == 31, (la, lb)[h], acc[6 + h])
        put_faces(lambda k: packed.at[t + 1, k], acc)
        for copy in sends(t + 1):
            copy.start()

        @pl.when(t == 0)
        def _():
            for copy in all_sends:
                copy.wait()

        @pl.when(t > 0)
        def _():
            f = t - 1
            near_field(
                f,
                lambda r: conc[f, pl.ds(pl.multiple_of(r, 8), 8), :],
                lambda k: arrived_all.at[k, f],
            )
            conc[f, 0:PAD, :] = jnp.concatenate(chosen_face(arrived_all.at[1, f], 1), axis=0)
            conc[f, PAD + ROWS : PAD + ROWS + PAD, :] = jnp.concatenate(
                chosen_face(arrived_all.at[0, f], 0), axis=0
            )

        for bit in range(8):

            @pl.when(t == bit)
            def _(bit=bit):
                flag_copy(bit).wait()

        flag[t + 1] = jnp.maximum(flag[t], flag_in[t])
        return carry

    lax.fori_loop(0, SWEEPS, sweep, 0)

    used = flag[SWEEPS]

    def bit_used(bit):
        return jnp.max(jnp.where(lane == bit, used, 0.0))

    inner = 0.0
    inner_any = 0.0
    for bit in range(6):
        on = bit_used(bit)
        inner = inner + on * bit
        inner_any = inner_any + on
    pick = jnp.where(inner_any > 0.0, 2.0 * inner + bit_used(7), 12.0)
    choice[0] = pick.astype(jnp.int32)

    copies = sends(SWEEPS)
    for k in range(2, 6):
        copies[k].wait_recv()
    near_field(
        FIELDS,
        lambda r: phi[0, pl.ds(pl.multiple_of(r, 8), 8), :],
        lambda k: arrived.at[SWEEPS, k],
    )
    activity = jnp.where(
        even,
        rate_const[0] * opened[0].astype(jnp.float32),
        rate_const[1] * opened[1].astype(jnp.float32),
    )
    give_first = jnp.full((8, 128), give_slot[0], jnp.int32) == 0
    rates = [diffusivity[i] for i in range(IONS)]

    def finish(x, carry):
        halves = []
        for h in range(2):
            r = pl.multiple_of(x * 16 + 8 * h, 8)
            rows = pl.ds(r, 8)
            inner_rows = pl.ds(pl.multiple_of(r + PAD, 8), 8)
            after = pl.ds(pl.multiple_of(r + 2 * PAD, 8), 8)

            def six(f, ref):
                return [ref(after), ref(rows)] + [near[f, n, rows, :] for n in range(4)]

            wet = conc[IONS, inner_rows, :]
            swept = phi[0, inner_rows, :]
            near_wet = six(IONS, lambda s: conc[IONS, s, :])
            near_swept = six(FIELDS, lambda s: phi[0, s, :])
            flow = drift = None
            weights = {1.0: [], 0.5: [], -0.5: []}
            for n in range(6):
                g = wet * near_wet[n]
                d = g * (swept - near_swept[n])
                half = 0.5 * d
                flow = g if flow is None else flow + g
                drift = d if drift is None else drift + d
                weights[1.0].append(g - d)
                weights[0.5].append(g - half)
                weights[-0.5].append(g + half)
            totals = {half: flow + half * drift for half in weights}
            ions = [conc[i, inner_rows, :] for i in range(IONS)]
            reaction = (
                activity
                * pore_in[rows, :].astype(jnp.float32)
                * (ions[2] - ions[0] * ions[1] * (1.0 / solubility))
            )
            out = []
            for i in range(IONS):
                half = 0.5 * valences[i]
                neighbours_of = six(i, lambda s, i=i: conc[i, s, :])
                outflow = ions[i] * totals[half]
                for n in range(6):
                    outflow = outflow - weights[half][n] * neighbours_of[n]
                value = ions[i] - rates[i] * outflow
                if reaction_signs[i] > 0:
                    value = value + reaction
                elif reaction_signs[i] < 0:
                    value = value - reaction
                updated[i, rows, :] = value
                out.append(value)
            updated[IONS, rows, :] = swept
            out.append(swept)
            halves.append(out)
        for i in range(FIELDS):
            a, b = halves[0][i], halves[1][i]
            outgoing[i, pl.ds(pl.multiple_of(x * 8, 8), 8), :] = jnp.where(
                even,
                jnp.where(give_first, a, sroll(a, 7)),
                jnp.where(give_first, sroll(b, 1), b),
            )
        return carry

    lax.fori_loop(1, SIDE - 1, finish, 0)
    for k in range(2):
        copies[k].wait_recv()
    for copy in copies:
        copy.wait_send()
    phi[0, 0:PAD, :] = jnp.concatenate(chosen_face(arrived.at[SWEEPS, 1], 1), axis=0)
    phi[0, PAD + ROWS : PAD + ROWS + PAD, :] = jnp.concatenate(
        chosen_face(arrived.at[SWEEPS, 0], 0), axis=0
    )
    lax.fori_loop(0, 2, lambda s, carry: finish(s * (SIDE - 1), carry), 0)


PAIRS = tuple((inner, outer) for inner in range(6) for outer in (6, 7)) + ((6, 7),)


def exchange_kernel(bits, outgoing, received, send_sems, recv_sems):
    group, dev = lax.axis_index("group"), lax.axis_index("dev")
    targets = [flipped(group, dev, bit) for bit in bits]
    barrier = pltpu.get_barrier_semaphore()
    for target in targets:
        pl.semaphore_signal(barrier, inc=1, device_id=target, device_id_type=MESH)
    pl.semaphore_wait(barrier, 2)
    copies = [
        pltpu.make_async_remote_copy(
            src_ref=outgoing.at[i],
            dst_ref=received.at[j, i],
            send_sem=send_sems.at[j, i],
            recv_sem=recv_sems.at[j, i],
            device_id=targets[j],
            device_id_type=MESH,
        )
        for i in range(FIELDS)
        for j in range(2)
    ]
    for copy in copies:
        copy.start()
    for copy in copies:
        copy.wait()


def exchange(outgoing, number):
    return pl.pallas_call(
        partial(exchange_kernel, PAIRS[number]),
        out_shape=jax.ShapeDtypeStruct((2, FIELDS, ROWS // 2, 128), jnp.float32),
        in_specs=[pl.BlockSpec(memory_space=pl.ANY)],
        out_specs=pl.BlockSpec(memory_space=pl.ANY),
        scratch_shapes=[pltpu.SemaphoreType.DMA((2, FIELDS))] * 2,
        compiler_params=pltpu.CompilerParams(collective_id=1 + number, has_side_effects=True),
        name=f"exchange_{number}",
    )(outgoing)


def merge_kernel(updated, received, control, new_species, new_potential):
    row, _ = iotas()
    even = row % 2 == 0
    first = control[0]
    give = control[1]
    swapped = control[2]
    give_first = jnp.full((8, 128), give, jnp.int32) == 0
    mine = (jnp.full((8, 128), swapped, jnp.int32) > 0) & (row % 2 == jnp.full((8, 128), give, jnp.int32))
    take_first = jnp.full((8, 128), first, jnp.int32) > 0

    def step(x, carry):
        for i in range(FIELDS):
            rows = pl.ds(pl.multiple_of(x * 8, 8), 8)
            got = jnp.where(take_first, received[0, i, rows, :], received[1, i, rows, :])
            halves = (
                jnp.where(give_first, got, sroll(got, 1)),
                jnp.where(give_first, sroll(got, 7), got),
            )
            for h in range(2):
                r = pl.ds(pl.multiple_of(x * 16 + 8 * h, 8), 8)
                value = jnp.where(mine, halves[h], updated[i, r, :])
                if i < IONS:
                    new_species[i, r, :] = value
                else:
                    new_potential[r, :] = value
        return carry

    lax.fori_loop(0, SIDE, step, 0)


def as_rows(field):
    lead = field.shape[:-2]
    split = field.reshape(lead + (2, ROWS // 2, 128))
    return jnp.swapaxes(split, -3, -2).reshape(lead + (ROWS, 128))


def as_bricks(rows):
    lead = rows.shape[:-2]
    split = rows.reshape(lead + (ROWS // 2, 2, 128))
    return jnp.swapaxes(split, -3, -2).reshape(lead + (2, ROWS // 2 * 128))


def local(
    species, potential, pore, openness, neighbours, diffusivity, rate_const, opened, partner, give_slot
):
    any_space = pl.BlockSpec(memory_space=pl.ANY)
    vmem = pl.BlockSpec(memory_space=pltpu.VMEM)
    smem = pl.BlockSpec(memory_space=pltpu.SMEM)
    f32 = jnp.float32
    padded = ROWS + 2 * PAD
    updated, outgoing, choice = pl.pallas_call(
        step_kernel,
        out_shape=(
            jax.ShapeDtypeStruct((FIELDS, ROWS, 128), f32),
            jax.ShapeDtypeStruct((FIELDS, ROWS // 2, 128), f32),
            jax.ShapeDtypeStruct((1,), jnp.int32),
        ),
        in_specs=[any_space] * 4 + [smem] * 6,
        out_specs=(vmem, vmem, smem),
        scratch_shapes=[
            pltpu.VMEM((2, padded, 128), f32),
            pltpu.VMEM((FIELDS, padded, 128), f32),
            pltpu.VMEM((FIELDS + 1, 4, ROWS, 128), f32),
            pltpu.VMEM((ROWS, 128), f32),
            pltpu.VMEM((ROWS, 128), jnp.int32),
            pltpu.VMEM((ROWS, 128), f32),
            pltpu.VMEM((SWEEPS + 1, 4, 16, 128), f32),
            pltpu.VMEM((SWEEPS + 1, 6, 16, 128), f32),
            pltpu.VMEM((4, FIELDS, 16, 128), f32),
            pltpu.VMEM((6, FIELDS, 16, 128), f32),
            pltpu.VMEM((SWEEPS + 1, 8, 128), f32),
            pltpu.VMEM((SWEEPS, 8, 128), f32),
            pltpu.SemaphoreType.DMA((3 + IONS,)),
            pltpu.SemaphoreType.DMA((SWEEPS + 1, 6)),
            pltpu.SemaphoreType.DMA((SWEEPS + 1, 6)),
            pltpu.SemaphoreType.DMA((6,)),
            pltpu.SemaphoreType.DMA((6,)),
            pltpu.SemaphoreType.DMA((SWEEPS,)),
            pltpu.SemaphoreType.DMA((SWEEPS,)),
        ],
        compiler_params=pltpu.CompilerParams(collective_id=0, has_side_effects=True),
        name="step",
    )(
        as_rows(potential),
        as_rows(pore),
        as_rows(openness),
        as_rows(species),
        neighbours,
        diffusivity,
        rate_const,
        opened,
        partner,
        give_slot,
    )
    received = lax.switch(
        choice[0], [partial(exchange, number=number) for number in range(len(PAIRS))], outgoing
    )
    me = lax.axis_index("group") * N_DEV + lax.axis_index("dev")
    apart = jnp.bitwise_xor(partner[0], me)
    first = (apart < 64) | ((apart == 64) & (choice[0] == len(PAIRS) - 1))
    control = jnp.stack([first.astype(jnp.int32), give_slot[0], (apart != 0).astype(jnp.int32)])
    new_species, new_potential = pl.pallas_call(
        merge_kernel,
        out_shape=(
            jax.ShapeDtypeStruct((IONS, ROWS, 128), f32),
            jax.ShapeDtypeStruct((ROWS, 128), f32),
        ),
        in_specs=[vmem, vmem, smem],
        out_specs=(vmem, vmem),
        name="merge",
    )(updated, received, control)
    return as_bricks(new_species), as_bricks(new_potential)


def solution(mesh):
    in_specs = (
        P(None, ("group", "dev"), None),
        P(("group", "dev"), None),
        P(("group", "dev"), None),
        P(("group", "dev"), None),
        P(("group", "dev"), None),
        P(),
        P(("group", "dev")),
        P(("group", "dev")),
        P(("group", "dev")),
        P(("group", "dev")),
    )
    out_specs = (P(None, ("group", "dev"), None), P(("group", "dev"), None))
    return jax.shard_map(local, mesh=mesh, in_specs=in_specs, out_specs=out_specs, check_vma=False)
```

```python
from functools import partial

import jax
import jax.numpy as jnp
from jax import lax
from jax.experimental import pallas as pl
from jax.experimental.pallas import tpu as pltpu
from jax.sharding import PartitionSpec as P

MESH = pl.DeviceIdType.MESH

SIDE = 32
SWEEPS = 8
ROWS = 512
PAD = 16
N_GROUP = 4
N_DEV = 64

charge_scale = 0.5
screening = 0.5
solubility = 2.0
valences = (2.0, -1.0, 1.0, -1.0, 1.0, 2.0)
reaction_signs = (1.0, 1.0, -1.0, 0.0, 0.0, 0.0)
IONS = len(valences)
FIELDS = IONS + 1
INV = 1.0 / (6.0 + screening)
MERGE_PARTS = 4


def iotas():
    row = lax.broadcasted_iota(jnp.int32, (8, 128), 0)
    lane = lax.broadcasted_iota(jnp.int32, (8, 128), 1)
    return row, lane


def lroll(v, shift):
    if isinstance(shift, int):
        shift %= 128
        return v if shift == 0 else pltpu.roll(v, shift, 1)
    return pltpu.roll(v, shift, 1)


def sroll(v, shift):
    shift %= 8
    return v if shift == 0 else pltpu.roll(v, shift, 0)


def flipped(group, dev, bit):
    q = group * N_DEV + dev
    mask = 2**bit
    other = q + (1 - 2 * ((q // mask) % 2)) * mask
    return {"group": other // N_DEV, "dev": other % N_DEV}


def plane_rows(x):
    return pl.multiple_of(x * 16, 16)


def pack_start():
    zero = jnp.zeros((8, 128), jnp.float32)
    return (zero,) * 8


def pack_planes(acc, xi, planes, row, lane):
    acc = list(acc)
    for j in range(2):
        low = high = None
        for i in range(4):
            a, b = planes[4 * j + i]
            first, last = sroll(a, 2 * i), sroll(b, 2 * i - 6)
            low = first if low is None else jnp.where(row // 2 == i, first, low)
            high = last if high is None else jnp.where(row // 2 == i, last, high)
        here = lane // 32 == xi
        acc[j] = jnp.where(here, lroll(low, 32 * xi), acc[j])
        acc[2 + j] = jnp.where(here, lroll(high, (32 * xi + 32) % 128), acc[2 + j])
    for i in range(8):
        x = 4 * i + xi
        z0, z1 = lane % 32 == x, lane % 32 == (x + 31) % 32
        for h in range(2):
            turned = lroll(planes[i][h], x)
            acc[4 + h] = jnp.where(z0, turned, acc[4 + h])
            acc[6 + h] = jnp.where(z1, turned, acc[6 + h])
    return tuple(acc)


def pack_end(acc):
    return acc[:6] + (lroll(acc[6], 97), lroll(acc[7], 97))


def around(a, b, x, i, turned, above, below, row, lane):
    north, south = turned
    ra, rb = lroll(a, 96), lroll(b, 96)
    ua, ub = sroll(ra, 6), sroll(rb, 6)
    edge = sroll(north[i // 4], 6 - 2 * (i % 4))
    na = jnp.where(lane < 96, ra, jnp.where(row < 6, ua, ub))
    nb = jnp.where(lane < 96, rb, jnp.where(row < 6, ub, edge))
    qa, qb = lroll(a, 32), lroll(b, 32)
    da, db = sroll(qa, 2), sroll(qb, 2)
    edge = sroll(south[i // 4], -2 * (i % 4))
    sa = jnp.where(lane >= 32, qa, jnp.where(row >= 2, da, edge))
    sb = jnp.where(lane >= 32, qb, jnp.where(row >= 2, db, da))
    top, bottom = lane % 32 == 31, lane % 32 == 0
    up = [jnp.where(top, lroll(above[h], 31 - x), lroll(v, 127)) for h, v in enumerate((a, b))]
    down = [
        jnp.where(bottom, lroll(below[h], (128 - x) % 128), lroll(v, 1)) for h, v in enumerate((a, b))
    ]
    return (na, sa, up[0], down[0]), (nb, sb, up[1], down[1])


def turn_faces(faces, xi):
    north = [lroll(v, (96 + 128 - 32 * xi) % 128) for v in faces[0]]
    south = [lroll(v, (128 - 32 * xi) % 128) for v in faces[1]]
    return north, south


def step_kernel(
    potential,
    pore,
    openness,
    species,
    neighbours,
    diffusivity,
    rate_const,
    opened,
    partner,
    give_slot,
    updated,
    outgoing,
    choice,
    control,
    phi,
    conc,
    near,
    dens,
    pore_in,
    open_in,
    packed,
    arrived,
    packed_all,
    arrived_all,
    flag,
    flag_in,
    load_sems,
    send_sems,
    recv_sems,
    send_all_sems,
    recv_all_sems,
    flag_send,
    flag_recv,
):
    row, lane = iotas()
    even = row % 2 == 0
    group, dev = lax.axis_index("group"), lax.axis_index("dev")
    loads = [
        pltpu.make_async_copy(potential, phi.at[0, pl.ds(PAD, ROWS)], load_sems.at[0]),
        pltpu.make_async_copy(pore, pore_in, load_sems.at[1]),
        pltpu.make_async_copy(openness, open_in, load_sems.at[2]),
    ] + [
        pltpu.make_async_copy(species.at[i], conc.at[i, pl.ds(PAD, ROWS)], load_sems.at[3 + i])
        for i in range(IONS)
    ]
    for load in loads:
        load.start()

    targets = [
        {"dev": (dev + N_DEV - 1) % N_DEV},
        {"dev": (dev + 1) % N_DEV},
        {"dev": (dev + N_DEV - 16) % N_DEV},
        {"dev": (dev + 16) % N_DEV},
        {"group": (group + N_GROUP - 1) % N_GROUP},
        {"group": (group + 1) % N_GROUP},
    ]
    flips = [flipped(group, dev, bit) for bit in range(8)]
    barrier = pltpu.get_barrier_semaphore()
    for target in targets + flips:
        pl.semaphore_signal(barrier, inc=1, device_id=target, device_id_type=MESH)

    keep = []
    for k in range(6):
        slots = jnp.where(even, neighbours[0, k], neighbours[1, k])
        keep.append(slots == row % 2)

    def chosen(k, v):
        return jnp.where(keep[k], v, jnp.where(even, sroll(v, 7), sroll(v, 1)))

    def chosen_face(ref, k):
        return [chosen(k, ref[0:8, :]), chosen(k, ref[8:16, :])]

    zeros = jnp.zeros((PAD, 128), jnp.float32)
    for s in range(2):
        phi[s, 0:PAD, :] = zeros
        phi[s, PAD + ROWS : PAD + ROWS + PAD, :] = zeros

    def sends(state):
        slot = state % 2
        sources = [phi.at[slot, pl.ds(PAD, 16)], phi.at[slot, pl.ds(ROWS, 16)]] + [
            packed.at[state, k - 2] for k in range(2, 6)
        ]
        return [
            pltpu.make_async_remote_copy(
                src_ref=sources[k],
                dst_ref=arrived.at[state, k],
                send_sem=send_sems.at[state, k],
                recv_sem=recv_sems.at[state, k],
                device_id=targets[k],
                device_id_type=MESH,
            )
            for k in range(6)
        ]

    def put_faces(ref_of, acc):
        for k in range(4):
            ref = ref_of(k)
            ref[0:8, :] = acc[2 * k]
            ref[8:16, :] = acc[2 * k + 1]

    def pack_field(read):
        def step(xi, acc):
            planes = []
            for i in range(8):
                r = plane_rows(4 * i + xi) + PAD
                planes.append((read(r), read(r + 8)))
            return pack_planes(acc, xi, planes, row, lane)

        return pack_end(lax.fori_loop(0, 4, step, pack_start(), unroll=4))

    loads[0].wait()
    acc = pack_field(lambda r: phi[0, pl.ds(pl.multiple_of(r, 8), 8), :])
    put_faces(lambda k: packed.at[0, k], acc)
    me = group * N_DEV + dev
    flag[0] = jnp.where(
        lane < 8,
        jnp.where(
            jnp.bitwise_xor(partner[0], me) == lax.shift_left(jnp.ones_like(lane), lane % 8), 1.0, 0.0
        ),
        0.0,
    )
    pl.semaphore_wait(barrier, len(targets) + len(flips))
    for copy in sends(0):
        copy.start()

    for load in loads[1:]:
        load.wait()

    def prepare(x, carry):
        for h in range(2):
            r = pl.multiple_of(x * 16 + 8 * h, 8)
            rows, inner = pl.ds(r, 8), pl.ds(pl.multiple_of(r + PAD, 8), 8)
            wet = pore_in[rows, :].astype(jnp.float32) * open_in[rows, :]
            conc[IONS, inner, :] = wet
            total = valences[0] * conc[0, inner, :]
            for i in range(1, IONS):
                total = total + valences[i] * conc[i, inner, :]
            dens[rows, :] = (charge_scale * INV) * wet * total
        return carry

    lax.fori_loop(0, SIDE, prepare, 0)

    def pack_one(f, carry):
        acc = pack_field(lambda r: conc[f, pl.ds(pl.multiple_of(r, 8), 8), :])
        put_faces(lambda k: packed_all.at[k, f], acc)
        return carry

    lax.fori_loop(0, FIELDS, pack_one, 0)
    sources = [conc.at[:, pl.ds(PAD, 16)], conc.at[:, pl.ds(ROWS, 16)]] + [
        packed_all.at[k] for k in range(4)
    ]
    all_sends = [
        pltpu.make_async_remote_copy(
            src_ref=sources[k],
            dst_ref=arrived_all.at[k],
            send_sem=send_all_sems.at[k],
            recv_sem=recv_all_sems.at[k],
            device_id=targets[k],
            device_id_type=MESH,
        )
        for k in range(6)
    ]
    for copy in all_sends:
        copy.start()

    def flag_copy(bit):
        return pltpu.make_async_remote_copy(
            src_ref=flag.at[bit],
            dst_ref=flag_in.at[bit],
            send_sem=flag_send.at[bit],
            recv_sem=flag_recv.at[bit],
            device_id=flips[bit],
            device_id_type=MESH,
        )

    def near_field(f, read, halo):
        faces = [chosen_face(halo(k), k) for k in range(2, 6)]

        def step(xi, carry):
            turned = turn_faces(faces[:2], xi)
            for i in range(8):
                x = 4 * i + xi
                r = plane_rows(x)
                a, b = read(r + PAD), read(r + PAD + 8)
                both = around(a, b, x, i, turned, faces[2], faces[3], row, lane)
                for h in range(2):
                    rows = pl.ds(pl.multiple_of(r + 8 * h, 8), 8)
                    for n in range(4):
                        near[f, n, rows, :] = both[h][n]
            return carry

        lax.fori_loop(0, 4, step, 0, unroll=4)

    def sweep(t, carry):
        old, new = t % 2, (t + 1) % 2
        for bit in range(8):

            @pl.when(t == bit)
            def _(bit=bit):
                flag_copy(bit).start()

        copies = sends(t)
        for k in range(2, 6):
            copies[k].wait_recv()
        faces = [chosen_face(arrived.at[t, k], k) for k in range(2, 6)]

        def read(r):
            return phi[old, pl.ds(pl.multiple_of(r, 8), 8), :]

        def step(xi, acc):
            turned = turn_faces(faces[:2], xi)
            planes = []
            for i in range(8):
                x = 4 * i + xi
                r = plane_rows(x)
                a, b = read(r + PAD), read(r + PAD + 8)
                both = around(a, b, x, i, turned, faces[2], faces[3], row, lane)
                out = []
                for h in range(2):
                    rows = pl.ds(pl.multiple_of(r + 8 * h, 8), 8)
                    total = read(r + 8 * h) + read(r + 8 * h + 2 * PAD)
                    for value in both[h]:
                        total = total + value
                    value = total * INV + dens[rows, :]
                    phi[new, pl.ds(pl.multiple_of(r + 8 * h + PAD, 8), 8), :] = value
                    out.append(value)
                planes.append(tuple(out))
            return pack_planes(acc, xi, planes, row, lane)

        acc = list(pack_end(lax.fori_loop(0, 4, step, pack_start(), unroll=4)))
        for k in range(2):
            copies[k].wait_recv()
        for copy in copies:
            copy.wait_send()
        ends = []
        for k, base in ((1, PAD), (0, ROWS)):
            halo = chosen_face(arrived.at[t, k], k)
            pair = []
            for h in range(2):
                value = phi[new, base + 8 * h : base + 8 * h + 8, :] + halo[h] * INV
                phi[new, base + 8 * h : base + 8 * h + 8, :] = value
                pair.append(value)
            ends.append(pair)
        (fa, fb), (la, lb) = ends
        first = (row < 2) & (lane < 32)
        last = (row >= 6) & (lane >= 96)
        acc[0] = jnp.where(first, fa, acc[0])
        acc[2] = jnp.where(first, lroll(sroll(fb, 2), 32), acc[2])
        acc[1] = jnp.where(last, lroll(sroll(la, 6), 96), acc[1])
        acc[3] = jnp.where(last, lb, acc[3])
        for h in range(2):
            acc[4 + h] = jnp.where(lane % 32 == 0, (fa, fb)[h], acc[4 + h])
            acc[4 + h] = jnp.where(lane % 32 == 31, lroll((la, lb)[h], 31), acc[4 + h])
            acc[6 + h] = jnp.where(lane % 32 == 0, lroll((fa, fb)[h], 97), acc[6 + h])
            acc[6 + h] = jnp.where(lane % 32 == 31, (la, lb)[h], acc[6 + h])
        put_faces(lambda k: packed.at[t + 1, k], acc)
        for copy in sends(t + 1):
            copy.start()

        @pl.when(t == 0)
        def _():
            for copy in all_sends:
                copy.wait()

        @pl.when(t > 0)
        def _():
            f = t - 1
            near_field(
                f,
                lambda r: conc[f, pl.ds(pl.multiple_of(r, 8), 8), :],
                lambda k: arrived_all.at[k, f],
            )
            conc[f, 0:PAD, :] = jnp.concatenate(chosen_face(arrived_all.at[1, f], 1), axis=0)
            conc[f, PAD + ROWS : PAD + ROWS + PAD, :] = jnp.concatenate(
                chosen_face(arrived_all.at[0, f], 0), axis=0
            )

        for bit in range(8):

            @pl.when(t == bit)
            def _(bit=bit):
                flag_copy(bit).wait()

        flag[t + 1] = jnp.maximum(flag[t], flag_in[t])
        return carry

    lax.fori_loop(0, SWEEPS, sweep, 0)

    used = flag[SWEEPS]

    def bit_used(bit):
        return jnp.max(jnp.where(lane == bit, used, 0.0))

    inner = 0.0
    inner_any = 0.0
    for bit in range(6):
        on = bit_used(bit)
        inner = inner + on * bit
        inner_any = inner_any + on
    pick = jnp.where(inner_any > 0.0, 2.0 * inner + bit_used(7), 12.0)
    choice[0] = pick.astype(jnp.int32)
    apart = jnp.bitwise_xor(partner[0], me)
    control[0] = jnp.where(apart == N_DEV, (pick == 12.0).astype(jnp.int32), (apart < N_DEV).astype(jnp.int32))
    control[1] = give_slot[0]
    control[2] = (apart != 0).astype(jnp.int32)

    copies = sends(SWEEPS)
    for k in range(2, 6):
        copies[k].wait_recv()
    near_field(
        FIELDS,
        lambda r: phi[0, pl.ds(pl.multiple_of(r, 8), 8), :],
        lambda k: arrived.at[SWEEPS, k],
    )
    activity = jnp.where(
        even,
        rate_const[0] * opened[0].astype(jnp.float32),
        rate_const[1] * opened[1].astype(jnp.float32),
    )
    give_first = jnp.full((8, 128), give_slot[0], jnp.int32) == 0
    rates = [diffusivity[i] for i in range(IONS)]

    def finish(x, carry):
        halves = []
        for h in range(2):
            r = pl.multiple_of(x * 16 + 8 * h, 8)
            rows = pl.ds(r, 8)
            inner_rows = pl.ds(pl.multiple_of(r + PAD, 8), 8)
            after = pl.ds(pl.multiple_of(r + 2 * PAD, 8), 8)

            def six(f, ref):
                return [ref(after), ref(rows)] + [near[f, n, rows, :] for n in range(4)]

            wet = conc[IONS, inner_rows, :]
            swept = phi[0, inner_rows, :]
            near_wet = six(IONS, lambda s: conc[IONS, s, :])
            near_swept = six(FIELDS, lambda s: phi[0, s, :])
            flow = drift = None
            weights = {1.0: [], 0.5: [], -0.5: []}
            for n in range(6):
                g = wet * near_wet[n]
                d = g * (swept - near_swept[n])
                half = 0.5 * d
                flow = g if flow is None else flow + g
                drift = d if drift is None else drift + d
                weights[1.0].append(g - d)
                weights[0.5].append(g - half)
                weights[-0.5].append(g + half)
            totals = {half: flow + half * drift for half in weights}
            ions = [conc[i, inner_rows, :] for i in range(IONS)]
            reaction = (
                activity
                * pore_in[rows, :].astype(jnp.float32)
                * (ions[2] - ions[0] * ions[1] * (1.0 / solubility))
            )
            out = []
            for i in range(IONS):
                half = 0.5 * valences[i]
                neighbours_of = six(i, lambda s, i=i: conc[i, s, :])
                outflow = ions[i] * totals[half]
                for n in range(6):
                    outflow = outflow - weights[half][n] * neighbours_of[n]
                value = ions[i] - rates[i] * outflow
                if reaction_signs[i] > 0:
                    value = value + reaction
                elif reaction_signs[i] < 0:
                    value = value - reaction
                updated[i, rows, :] = value
                out.append(value)
            updated[IONS, rows, :] = swept
            out.append(swept)
            halves.append(out)
        for i in range(FIELDS):
            a, b = halves[0][i], halves[1][i]
            outgoing[i, pl.ds(pl.multiple_of(x * 8, 8), 8), :] = jnp.where(
                even,
                jnp.where(give_first, a, sroll(a, 7)),
                jnp.where(give_first, sroll(b, 1), b),
            )
        return carry

    lax.fori_loop(1, SIDE - 1, finish, 0)
    for k in range(2):
        copies[k].wait_recv()
    for copy in copies:
        copy.wait_send()
    phi[0, 0:PAD, :] = jnp.concatenate(chosen_face(arrived.at[SWEEPS, 1], 1), axis=0)
    phi[0, PAD + ROWS : PAD + ROWS + PAD, :] = jnp.concatenate(
        chosen_face(arrived.at[SWEEPS, 0], 0), axis=0
    )
    lax.fori_loop(0, 2, lambda s, carry: finish(s * (SIDE - 1), carry), 0)


PAIRS = tuple((inner, outer) for inner in range(6) for outer in (6, 7)) + ((6, 7),)


def exchange_kernel(bits, outgoing, received, send_sems, recv_sems):
    group, dev = lax.axis_index("group"), lax.axis_index("dev")
    targets = [flipped(group, dev, bit) for bit in bits]
    barrier = pltpu.get_barrier_semaphore()
    for target in targets:
        pl.semaphore_signal(barrier, inc=1, device_id=target, device_id_type=MESH)
    pl.semaphore_wait(barrier, 2)
    copies = [
        pltpu.make_async_remote_copy(
            src_ref=outgoing.at[i],
            dst_ref=received.at[j, i],
            send_sem=send_sems.at[j, i],
            recv_sem=recv_sems.at[j, i],
            device_id=targets[j],
            device_id_type=MESH,
        )
        for i in range(FIELDS)
        for j in range(2)
    ]
    for copy in copies:
        copy.start()
    for copy in copies:
        copy.wait()


def exchange(outgoing, number):
    return pl.pallas_call(
        partial(exchange_kernel, PAIRS[number]),
        out_shape=jax.ShapeDtypeStruct((2, FIELDS, ROWS // 2, 128), jnp.float32),
        in_specs=[pl.BlockSpec(memory_space=pl.ANY)],
        out_specs=pl.BlockSpec(memory_space=pl.ANY),
        scratch_shapes=[pltpu.SemaphoreType.DMA((2, FIELDS))] * 2,
        compiler_params=pltpu.CompilerParams(
            collective_id=1 + number, has_side_effects=True
        ),
        name=f"exchange_{number}",
    )(outgoing)


def merge_kernel(updated, received, control, new_species, new_potential, ions, field, sems):
    row, _ = iotas()
    even = row % 2 == 0
    first = control[0]
    give = control[1]
    swapped = control[2]
    give_first = jnp.full((8, 128), give, jnp.int32) == 0
    mine = (jnp.full((8, 128), swapped, jnp.int32) > 0) & (row % 2 == jnp.full((8, 128), give, jnp.int32))
    take_first = jnp.full((8, 128), first, jnp.int32) > 0

    def step(x, carry):
        for i in range(FIELDS):
            rows = pl.ds(pl.multiple_of(x * 8, 8), 8)
            got = jnp.where(take_first, received[0, i, rows, :], received[1, i, rows, :])
            halves = (
                jnp.where(give_first, got, sroll(got, 1)),
                jnp.where(give_first, sroll(got, 7), got),
            )
            for h in range(2):
                r = pl.ds(pl.multiple_of(x * 16 + 8 * h, 8), 8)
                value = jnp.where(mine, halves[h], updated[i, r, :])
                if i < IONS:
                    ions[i, r, :] = value
                else:
                    field[r, :] = value
        return carry

    copies = []
    part = ROWS // MERGE_PARTS
    for n in range(MERGE_PARTS):
        lax.fori_loop(n * SIDE // MERGE_PARTS, (n + 1) * SIDE // MERGE_PARTS, step, 0, unroll=2)
        rows = pl.ds(n * part, part)
        pair = [
            pltpu.make_async_copy(ions.at[:, rows], new_species.at[:, rows], sems.at[n, 0]),
            pltpu.make_async_copy(field.at[rows], new_potential.at[rows], sems.at[n, 1]),
        ]
        for copy in pair:
            copy.start()
        copies += pair
    for copy in copies:
        copy.wait()


def as_rows(field):
    lead = field.shape[:-2]
    split = field.reshape(lead + (2, ROWS // 2, 128))
    return jnp.swapaxes(split, -3, -2).reshape(lead + (ROWS, 128))


def as_bricks(rows):
    lead = rows.shape[:-2]
    split = rows.reshape(lead + (ROWS // 2, 2, 128))
    return jnp.swapaxes(split, -3, -2).reshape(lead + (2, ROWS // 2 * 128))


def local(
    species, potential, pore, openness, neighbours, diffusivity, rate_const, opened, partner, give_slot
):
    hbm = pl.BlockSpec(memory_space=pl.ANY)
    vmem = pl.BlockSpec(memory_space=pltpu.VMEM)
    smem = pl.BlockSpec(memory_space=pltpu.SMEM)
    f32 = jnp.float32
    padded = ROWS + 2 * PAD
    updated, outgoing, choice, control = pl.pallas_call(
        step_kernel,
        out_shape=(
            jax.ShapeDtypeStruct((FIELDS, ROWS, 128), f32),
            jax.ShapeDtypeStruct((FIELDS, ROWS // 2, 128), f32),
            jax.ShapeDtypeStruct((1,), jnp.int32),
            jax.ShapeDtypeStruct((3,), jnp.int32),
        ),
        in_specs=[hbm] * 4 + [smem] * 6,
        out_specs=(vmem, vmem, smem, smem),
        scratch_shapes=[
            pltpu.VMEM((2, padded, 128), f32),
            pltpu.VMEM((FIELDS, padded, 128), f32),
            pltpu.VMEM((FIELDS + 1, 4, ROWS, 128), f32),
            pltpu.VMEM((ROWS, 128), f32),
            pltpu.VMEM((ROWS, 128), jnp.int32),
            pltpu.VMEM((ROWS, 128), f32),
            pltpu.VMEM((SWEEPS + 1, 4, 16, 128), f32),
            pltpu.VMEM((SWEEPS + 1, 6, 16, 128), f32),
            pltpu.VMEM((4, FIELDS, 16, 128), f32),
            pltpu.VMEM((6, FIELDS, 16, 128), f32),
            pltpu.VMEM((SWEEPS + 1, 8, 128), f32),
            pltpu.VMEM((SWEEPS, 8, 128), f32),
            pltpu.SemaphoreType.DMA((3 + IONS,)),
            pltpu.SemaphoreType.DMA((SWEEPS + 1, 6)),
            pltpu.SemaphoreType.DMA((SWEEPS + 1, 6)),
            pltpu.SemaphoreType.DMA((6,)),
            pltpu.SemaphoreType.DMA((6,)),
            pltpu.SemaphoreType.DMA((SWEEPS,)),
            pltpu.SemaphoreType.DMA((SWEEPS,)),
        ],
        compiler_params=pltpu.CompilerParams(
            collective_id=0, has_side_effects=True
        ),
        name="step",
    )(
        as_rows(potential),
        as_rows(pore),
        as_rows(openness),
        as_rows(species),
        neighbours,
        diffusivity,
        rate_const,
        opened,
        partner,
        give_slot,
    )
    received = lax.switch(
        choice[0], [partial(exchange, number=number) for number in range(len(PAIRS))], outgoing
    )
    new_species, new_potential = pl.pallas_call(
        merge_kernel,
        out_shape=(
            jax.ShapeDtypeStruct((IONS, ROWS, 128), f32),
            jax.ShapeDtypeStruct((ROWS, 128), f32),
        ),
        in_specs=[vmem, vmem, smem],
        out_specs=(hbm, hbm),
        scratch_shapes=[
            pltpu.VMEM((IONS, ROWS, 128), f32),
            pltpu.VMEM((ROWS, 128), f32),
            pltpu.SemaphoreType.DMA((MERGE_PARTS, 2)),
        ],
        name="merge",
    )(updated, received, control)
    return as_bricks(new_species), as_bricks(new_potential)


def solution(mesh):
    in_specs = (
        P(None, ("group", "dev"), None),
        P(("group", "dev"), None),
        P(("group", "dev"), None),
        P(("group", "dev"), None),
        P(("group", "dev"), None),
        P(),
        P(("group", "dev")),
        P(("group", "dev")),
        P(("group", "dev")),
        P(("group", "dev")),
    )
    out_specs = (P(None, ("group", "dev"), None), P(("group", "dev"), None))
    return jax.shard_map(local, mesh=mesh, in_specs=in_specs, out_specs=out_specs, check_vma=False)
```

```python
from functools import partial

import jax
import jax.numpy as jnp
from jax import lax
from jax.experimental import pallas as pl
from jax.experimental.pallas import tpu as pltpu
from jax.sharding import PartitionSpec as P

MESH = pl.DeviceIdType.MESH

SIDE = 32
SWEEPS = 8
ROWS = 512
PAD = 16
N_GROUP = 4
N_DEV = 64

charge_scale = 0.5
screening = 0.5
solubility = 2.0
valences = (2.0, -1.0, 1.0, -1.0, 1.0, 2.0)
reaction_signs = (1.0, 1.0, -1.0, 0.0, 0.0, 0.0)
IONS = len(valences)
FIELDS = IONS + 1
INV = 1.0 / (6.0 + screening)
FIRST = 2
SHARE = 312


def iotas():
    row = lax.broadcasted_iota(jnp.int32, (8, 128), 0)
    lane = lax.broadcasted_iota(jnp.int32, (8, 128), 1)
    return row, lane


def lroll(v, shift):
    if isinstance(shift, int):
        shift %= 128
        return v if shift == 0 else pltpu.roll(v, shift, 1)
    return pltpu.roll(v, shift, 1)


def sroll(v, shift):
    shift %= 8
    return v if shift == 0 else pltpu.roll(v, shift, 0)


def flipped(group, dev, bit):
    q = group * N_DEV + dev
    mask = 2**bit
    other = q + (1 - 2 * ((q // mask) % 2)) * mask
    return {"group": other // N_DEV, "dev": other % N_DEV}


def plane_rows(x):
    return pl.multiple_of(x * 16, 16)


def pack_start():
    zero = jnp.zeros((8, 128), jnp.float32)
    return (zero,) * 8


def pack_planes(acc, xi, planes, row, lane):
    acc = list(acc)
    for j in range(2):
        low = high = None
        for i in range(4):
            a, b = planes[4 * j + i]
            first, last = sroll(a, 2 * i), sroll(b, 2 * i - 6)
            low = first if low is None else jnp.where(row // 2 == i, first, low)
            high = last if high is None else jnp.where(row // 2 == i, last, high)
        here = lane // 32 == xi
        acc[j] = jnp.where(here, lroll(low, 32 * xi), acc[j])
        acc[2 + j] = jnp.where(here, lroll(high, (32 * xi + 32) % 128), acc[2 + j])
    for i in range(8):
        x = 4 * i + xi
        z0, z1 = lane % 32 == x, lane % 32 == (x + 31) % 32
        for h in range(2):
            turned = lroll(planes[i][h], x)
            acc[4 + h] = jnp.where(z0, turned, acc[4 + h])
            acc[6 + h] = jnp.where(z1, turned, acc[6 + h])
    return tuple(acc)


def pack_end(acc):
    return acc[:6] + (lroll(acc[6], 97), lroll(acc[7], 97))


def around(a, b, x, i, turned, above, below, row, lane):
    north, south = turned
    ra, rb = lroll(a, 96), lroll(b, 96)
    ua, ub = sroll(ra, 6), sroll(rb, 6)
    edge = sroll(north[i // 4], 6 - 2 * (i % 4))
    na = jnp.where(lane < 96, ra, jnp.where(row < 6, ua, ub))
    nb = jnp.where(lane < 96, rb, jnp.where(row < 6, ub, edge))
    qa, qb = lroll(a, 32), lroll(b, 32)
    da, db = sroll(qa, 2), sroll(qb, 2)
    edge = sroll(south[i // 4], -2 * (i % 4))
    sa = jnp.where(lane >= 32, qa, jnp.where(row >= 2, da, edge))
    sb = jnp.where(lane >= 32, qb, jnp.where(row >= 2, db, da))
    top, bottom = lane % 32 == 31, lane % 32 == 0
    up = [jnp.where(top, lroll(above[h], 31 - x), lroll(v, 127)) for h, v in enumerate((a, b))]
    down = [
        jnp.where(bottom, lroll(below[h], (128 - x) % 128), lroll(v, 1)) for h, v in enumerate((a, b))
    ]
    return (na, sa, up[0], down[0]), (nb, sb, up[1], down[1])


def turn_faces(faces, xi):
    north = [lroll(v, (96 + 128 - 32 * xi) % 128) for v in faces[0]]
    south = [lroll(v, (128 - 32 * xi) % 128) for v in faces[1]]
    return north, south


def neighbour_targets(group, dev):
    return [
        {"dev": (dev + N_DEV - 1) % N_DEV},
        {"dev": (dev + 1) % N_DEV},
        {"dev": (dev + N_DEV - 16) % N_DEV},
        {"dev": (dev + 16) % N_DEV},
        {"group": (group + N_GROUP - 1) % N_GROUP},
        {"group": (group + 1) % N_GROUP},
    ]


def chooser(neighbours, row):
    even = row % 2 == 0
    keep = []
    for k in range(6):
        slots = jnp.where(even, neighbours[0, k], neighbours[1, k])
        keep.append(slots == row % 2)

    def chosen_face(ref, k):
        return [
            jnp.where(keep[k], v, jnp.where(even, sroll(v, 7), sroll(v, 1)))
            for v in (ref[0:8, :], ref[8:16, :])
        ]

    return chosen_face


def eight(r):
    return pl.ds(pl.multiple_of(r, 8), 8)


def put_faces(ref_of, acc):
    for k in range(4):
        ref = ref_of(k)
        ref[0:8, :] = acc[2 * k]
        ref[8:16, :] = acc[2 * k + 1]


def face_sends(state, base, phi, packed, arrived, send_sems, recv_sems, targets):
    slot, n = state % 2, state - base
    sources = [phi.at[slot, pl.ds(PAD, 16)], phi.at[slot, pl.ds(ROWS, 16)]] + [
        packed.at[n, k] for k in range(4)
    ]
    return [
        pltpu.make_async_remote_copy(
            src_ref=sources[k],
            dst_ref=arrived.at[n, k],
            send_sem=send_sems.at[n, k],
            recv_sem=recv_sems.at[n, k],
            device_id=targets[k],
            device_id_type=MESH,
        )
        for k in range(6)
    ]


def sweep_once(t, base, phi, dens, packed, arrived, copies, chosen_face, row, lane):
    old, new = t % 2, (t + 1) % 2
    for k in range(2, 6):
        copies[k].wait_recv()
    faces = [chosen_face(arrived.at[t - base, k], k) for k in range(2, 6)]

    def step(xi, acc):
        turned = turn_faces(faces[:2], xi)
        planes = []
        for i in range(8):
            x = 4 * i + xi
            r = plane_rows(x)
            a, b = phi[old, eight(r + PAD), :], phi[old, eight(r + PAD + 8), :]
            both = around(a, b, x, i, turned, faces[2], faces[3], row, lane)
            out = []
            for h in range(2):
                total = phi[old, eight(r + 8 * h), :] + phi[old, eight(r + 8 * h + 2 * PAD), :]
                for value in both[h]:
                    total = total + value
                value = total * INV + dens[eight(r + 8 * h), :]
                phi[new, eight(r + 8 * h + PAD), :] = value
                out.append(value)
            planes.append(tuple(out))
        return pack_planes(acc, xi, planes, row, lane)

    acc = list(pack_end(lax.fori_loop(0, 4, step, pack_start(), unroll=4)))
    for k in range(2):
        copies[k].wait_recv()
    for copy in copies:
        copy.wait_send()
    ends = []
    for k, start in ((1, PAD), (0, ROWS)):
        halo = chosen_face(arrived.at[t - base, k], k)
        pair = []
        for h in range(2):
            value = phi[new, start + 8 * h : start + 8 * h + 8, :] + halo[h] * INV
            phi[new, start + 8 * h : start + 8 * h + 8, :] = value
            pair.append(value)
        ends.append(pair)
    (fa, fb), (la, lb) = ends
    first = (row < 2) & (lane < 32)
    last = (row >= 6) & (lane >= 96)
    acc[0] = jnp.where(first, fa, acc[0])
    acc[2] = jnp.where(first, lroll(sroll(fb, 2), 32), acc[2])
    acc[1] = jnp.where(last, lroll(sroll(la, 6), 96), acc[1])
    acc[3] = jnp.where(last, lb, acc[3])
    for h in range(2):
        acc[4 + h] = jnp.where(lane % 32 == 0, (fa, fb)[h], acc[4 + h])
        acc[4 + h] = jnp.where(lane % 32 == 31, lroll((la, lb)[h], 31), acc[4 + h])
        acc[6 + h] = jnp.where(lane % 32 == 0, lroll((fa, fb)[h], 97), acc[6 + h])
        acc[6 + h] = jnp.where(lane % 32 == 31, (la, lb)[h], acc[6 + h])
    put_faces(lambda k: packed.at[t + 1 - base, k], acc)


def open_kernel(
    potential,
    pore,
    openness,
    species,
    neighbours,
    partner,
    give_slot,
    phi_out,
    conc_out,
    dens_out,
    faces_out,
    packed_out,
    choice,
    control,
    phi,
    conc,
    dens,
    pore_in,
    open_in,
    packed,
    arrived,
    packed_all,
    arrived_all,
    flag,
    flag_in,
    load_sems,
    out_sems,
    send_sems,
    recv_sems,
    send_all_sems,
    recv_all_sems,
    flag_send,
    flag_recv,
):
    row, lane = iotas()
    group, dev = lax.axis_index("group"), lax.axis_index("dev")
    loads = [
        pltpu.make_async_copy(potential, phi.at[0, pl.ds(PAD, ROWS)], load_sems.at[0]),
        pltpu.make_async_copy(pore, pore_in, load_sems.at[1]),
        pltpu.make_async_copy(openness, open_in, load_sems.at[2]),
    ] + [
        pltpu.make_async_copy(species.at[i], conc.at[i, pl.ds(PAD, ROWS)], load_sems.at[3 + i])
        for i in range(IONS)
    ]
    for load in loads:
        load.start()
    targets = neighbour_targets(group, dev)
    near_targets = [{"dev": dev // 16 * 16 + (dev % 16 + i) % 16} for i in range(1, 16)]
    far_targets = [
        {"group": (group + i // 4) % N_GROUP, "dev": (dev + 16 * (i % 4)) % N_DEV} for i in range(1, 16)
    ]
    barrier = pltpu.get_barrier_semaphore()
    everyone = targets + near_targets + far_targets
    for target in everyone:
        pl.semaphore_signal(barrier, inc=1, device_id=target, device_id_type=MESH)
    chosen_face = chooser(neighbours, row)

    zeros = jnp.zeros((PAD, 128), jnp.float32)
    for s in range(2):
        phi[s, 0:PAD, :] = zeros
        phi[s, PAD + ROWS : PAD + ROWS + PAD, :] = zeros

    def sends(state):
        return face_sends(state, 0, phi, packed, arrived, send_sems, recv_sems, targets)

    def pack_field(read):
        def step(xi, acc):
            planes = []
            for i in range(8):
                r = plane_rows(4 * i + xi) + PAD
                planes.append((read(r), read(r + 8)))
            return pack_planes(acc, xi, planes, row, lane)

        return pack_end(lax.fori_loop(0, 4, step, pack_start(), unroll=4))

    loads[0].wait()
    acc = pack_field(lambda r: phi[0, eight(r), :])
    put_faces(lambda k: packed.at[0, k], acc)
    me = group * N_DEV + dev
    apart = jnp.bitwise_xor(partner[0], me)
    flag[0] = jnp.where(
        lane < 8,
        jnp.where(apart == lax.shift_left(jnp.ones_like(lane), lane % 8), 1.0, 0.0),
        0.0,
    )
    pl.semaphore_wait(barrier, len(everyone))
    for copy in sends(0):
        copy.start()

    def flag_copies(stage):
        return [
            pltpu.make_async_remote_copy(
                src_ref=flag.at[stage, pl.ds(0, 1)],
                dst_ref=flag_in.at[stage, i, pl.ds(0, 1)],
                send_sem=flag_send.at[stage, i],
                recv_sem=flag_recv.at[stage, i],
                device_id=target,
                device_id_type=MESH,
            )
            for i, target in enumerate((near_targets, far_targets)[stage])
        ]

    def flag_join(stage):
        for copy in flag_copies(stage):
            copy.wait()
        total = flag[stage, 0:1, :]
        for i in range(15):
            total = jnp.maximum(total, flag_in[stage, i, 0:1, :])
        return total

    for copy in flag_copies(0):
        copy.start()
    for load in loads[1:]:
        load.wait()

    def prepare(x, carry):
        for h in range(2):
            r = x * 16 + 8 * h
            rows, inner = eight(r), eight(r + PAD)
            wet = pore_in[rows, :].astype(jnp.float32) * open_in[rows, :]
            conc[IONS, inner, :] = wet
            total = valences[0] * conc[0, inner, :]
            for i in range(1, IONS):
                total = total + valences[i] * conc[i, inner, :]
            dens[rows, :] = (charge_scale * INV) * wet * total
        return carry

    lax.fori_loop(0, SIDE, prepare, 0, unroll=2)
    outs = [pltpu.make_async_copy(dens, dens_out, out_sems.at[0])]
    outs[0].start()

    def pack_one(f, carry):
        acc = pack_field(lambda r: conc[f, eight(r), :])
        put_faces(lambda k: packed_all.at[k, f], acc)
        return carry

    lax.fori_loop(0, FIELDS, pack_one, 0)
    sources = [conc.at[:, pl.ds(PAD, 16)], conc.at[:, pl.ds(ROWS, 16)]] + [
        packed_all.at[k] for k in range(4)
    ]
    all_sends = [
        pltpu.make_async_remote_copy(
            src_ref=sources[k],
            dst_ref=arrived_all.at[k],
            send_sem=send_all_sems.at[k],
            recv_sem=recv_all_sems.at[k],
            device_id=targets[k],
            device_id_type=MESH,
        )
        for k in range(6)
    ]
    for copy in all_sends:
        copy.start()
    late = [
        pltpu.make_async_copy(conc, conc_out, out_sems.at[1]),
        pltpu.make_async_copy(arrived_all, faces_out, out_sems.at[2]),
    ]

    def sweep(t, carry):
        sweep_once(t, 0, phi, dens, packed, arrived, sends(t), chosen_face, row, lane)

        @pl.when(t == 0)
        def _():
            for copy in sends(1):
                copy.start()
            flag[1, 0:1, :] = flag_join(0)
            for copy in flag_copies(1):
                copy.start()
            for copy in all_sends:
                copy.wait()
            for f in range(FIELDS):
                for k, start in ((1, 0), (0, PAD + ROWS)):
                    a, b = chosen_face(arrived_all.at[k, f], k)
                    conc[f, start : start + 8, :] = a
                    conc[f, start + 8 : start + 16, :] = b
            for copy in late:
                copy.start()

        return carry

    lax.fori_loop(0, FIRST, sweep, 0)
    last = [
        pltpu.make_async_copy(phi.at[FIRST % 2], phi_out, out_sems.at[3]),
        pltpu.make_async_copy(packed.at[FIRST], packed_out, out_sems.at[4]),
    ]
    for copy in last:
        copy.start()

    used = flag_join(1)
    place = lane[0:1, :]

    def bit_used(bit):
        return jnp.max(jnp.where(place == bit, used, 0.0))

    inner = 0.0
    inner_any = 0.0
    for bit in range(6):
        on = bit_used(bit)
        inner = inner + on * bit
        inner_any = inner_any + on
    pick = jnp.where(inner_any > 0.0, 2.0 * inner + bit_used(7), 12.0)
    choice[0] = pick.astype(jnp.int32)
    control[0] = jnp.where(apart == N_DEV, (pick == 12.0).astype(jnp.int32), (apart < N_DEV).astype(jnp.int32))
    control[1] = give_slot[0]
    control[2] = (apart != 0).astype(jnp.int32)
    for copy in outs + late + last:
        copy.wait()


PAIRS = tuple((inner, outer) for inner in range(6) for outer in (6, 7)) + ((6, 7),)


def close_kernel(
    bits,
    phi_first,
    conc_first,
    dens_first,
    faces_first,
    packed_first,
    neighbours,
    diffusivity,
    rate_const,
    opened,
    control,
    updated,
    relaxed,
    phi,
    conc,
    near,
    dens,
    faces_all,
    packed,
    arrived,
    share,
    share_in,
    load_sems,
    send_sems,
    recv_sems,
    share_send,
    share_recv,
):
    row, lane = iotas()
    even = row % 2 == 0
    group, dev = lax.axis_index("group"), lax.axis_index("dev")
    loads = [
        pltpu.make_async_copy(phi_first, phi.at[FIRST % 2], load_sems.at[0]),
        pltpu.make_async_copy(packed_first, packed.at[0], load_sems.at[1]),
        pltpu.make_async_copy(conc_first, conc.at[pl.ds(0, FIELDS)], load_sems.at[2]),
        pltpu.make_async_copy(faces_first, faces_all.at[:, pl.ds(0, FIELDS)], load_sems.at[3]),
        pltpu.make_async_copy(dens_first, dens, load_sems.at[4]),
    ]
    for load in loads:
        load.start()
    targets = neighbour_targets(group, dev)
    partners = [flipped(group, dev, bit) for bit in bits]
    barrier = pltpu.get_barrier_semaphore()
    for target in targets + partners:
        pl.semaphore_signal(barrier, inc=1, device_id=target, device_id_type=MESH)
    chosen_face = chooser(neighbours, row)
    give = jnp.full((8, 128), control[1], jnp.int32)
    give_first = give == 0
    take_first = jnp.full((8, 128), control[0], jnp.int32) > 0
    mine = (jnp.full((8, 128), control[2], jnp.int32) > 0) & (row % 2 == give)

    def folded(a, b):
        return jnp.where(
            even,
            jnp.where(give_first, a, sroll(a, 7)),
            jnp.where(give_first, sroll(b, 1), b),
        )

    def merged(f, r, a, b):
        got = jnp.where(take_first, share_in[0, f, eight(r), :], share_in[1, f, eight(r), :])
        return (
            jnp.where(mine, jnp.where(give_first, got, sroll(got, 1)), a),
            jnp.where(mine, jnp.where(give_first, sroll(got, 7), got), b),
        )

    zeros = jnp.zeros((PAD, 128), jnp.float32)
    other = (FIRST + 1) % 2
    phi[other, 0:PAD, :] = zeros
    phi[other, PAD + ROWS : PAD + ROWS + PAD, :] = zeros

    def sends(state):
        return face_sends(state, FIRST, phi, packed, arrived, send_sems, recv_sems, targets)

    def share_copies(f, start, size, sem):
        return [
            pltpu.make_async_remote_copy(
                src_ref=share.at[f, pl.ds(start, size)],
                dst_ref=share_in.at[j, f, pl.ds(start, size)],
                send_sem=share_send.at[j, sem],
                recv_sem=share_recv.at[j, sem],
                device_id=target,
                device_id_type=MESH,
            )
            for j, target in enumerate(partners)
        ]

    def field_faces(f):
        return [chosen_face(faces_all.at[k, f], k) for k in range(2, 6)]

    def fold_edges(f):
        for r, start in ((256, 0), (264, PAD + ROWS)):
            share[f, r : r + 8, :] = folded(conc[f, start : start + 8, :], conc[f, start + 8 : start + 16, :])
        faces = field_faces(f)
        for k in range(4):
            share[f, 272 + 8 * k : 280 + 8 * k, :] = folded(*faces[k])

    def share_field(f, carry):
        def step(x, carry):
            r = plane_rows(x) + PAD
            share[f, eight(x * 8), :] = folded(conc[f, eight(r), :], conc[f, eight(r + 8), :])
            return carry

        lax.fori_loop(0, SIDE, step, 0, unroll=4)

        @pl.when(f < FIELDS)
        def _():
            fold_edges(f)
            for copy in share_copies(f, 0, 304, f):
                copy.start()

        @pl.when(f == FIELDS)
        def _():
            for copy in share_copies(FIELDS, 0, 256, FIELDS):
                copy.start()

        return carry

    def take_field(f):
        @pl.when(f < FIELDS)
        def _():
            for copy in share_copies(f, 0, 304, f):
                copy.wait()

        @pl.when(f == FIELDS)
        def _():
            for copy in share_copies(FIELDS, 0, 256, FIELDS) + share_copies(FIELDS, 256, 56, FIELDS + 1):
                copy.wait()

        def step(x, carry):
            r = plane_rows(x) + PAD
            a, b = merged(f, x * 8, conc[f, eight(r), :], conc[f, eight(r + 8), :])
            conc[f, eight(r), :] = a
            conc[f, eight(r + 8), :] = b
            return carry

        lax.fori_loop(0, SIDE, step, 0, unroll=4)
        for r, start in ((256, 0), (264, PAD + ROWS)):
            a, b = merged(f, r, conc[f, start : start + 8, :], conc[f, start + 8 : start + 16, :])
            conc[f, start : start + 8, :] = a
            conc[f, start + 8 : start + 16, :] = b
        faces = [merged(f, 272 + 8 * k, *face) for k, face in enumerate(field_faces(f))]

        def spread(xi, carry):
            turned = turn_faces(faces[:2], xi)
            for i in range(8):
                x = 4 * i + xi
                r = plane_rows(x)
                a, b = conc[f, eight(r + PAD), :], conc[f, eight(r + PAD + 8), :]
                both = around(a, b, x, i, turned, faces[2], faces[3], row, lane)
                for h in range(2):
                    for n in range(4):
                        near[f, n, eight(r + 8 * h), :] = both[h][n]
            return carry

        lax.fori_loop(0, 4, spread, 0, unroll=4)

    for load in loads[:2]:
        load.wait()
    pl.semaphore_wait(barrier, len(targets) + len(partners))
    for copy in sends(FIRST):
        copy.start()
    for load in loads[2:]:
        load.wait()
    activity = jnp.where(
        even,
        rate_const[0] * opened[0].astype(jnp.float32),
        rate_const[1] * opened[1].astype(jnp.float32),
    )
    share[FIELDS, 304:312, :] = folded(activity, activity)
    lag = 4

    def step(t, carry):
        @pl.when(t == SWEEPS)
        def _():
            def move(x, carry):
                conc[FIELDS, eight(x * 8 + PAD), :] = phi[SWEEPS % 2, eight(x * 8 + PAD), :]
                return carry

            lax.fori_loop(0, ROWS // 8, move, 0, unroll=8)

        @pl.when(t <= SWEEPS)
        def _():
            lax.fori_loop((t - 1) * jnp.minimum(t - FIRST, 1), t, share_field, 0)

        @pl.when(t == SWEEPS + 2)
        def _():
            for copy in sends(SWEEPS):
                copy.wait()
            for k in range(2, 6):
                faces_all[k, FIELDS] = arrived[SWEEPS - FIRST, k]
            for k, start in ((1, 0), (0, PAD + ROWS)):
                a, b = chosen_face(arrived.at[SWEEPS - FIRST, k], k)
                conc[FIELDS, start : start + 8, :] = a
                conc[FIELDS, start + 8 : start + 16, :] = b
            fold_edges(FIELDS)
            for copy in share_copies(FIELDS, 256, 56, FIELDS + 1):
                copy.start()

        @pl.when(t >= lag)
        def _():
            take_field(t - lag)

        @pl.when(t < SWEEPS)
        def _():
            sweep_once(t, FIRST, phi, dens, packed, arrived, sends(t), chosen_face, row, lane)
            for copy in sends(t + 1):
                copy.start()

        return carry

    lax.fori_loop(FIRST, FIELDS + 1 + lag, step, 0)
    activity = merged(FIELDS, 304, activity, activity)[0]
    rates = [diffusivity[i] for i in range(IONS)]

    def finish(x, carry):
        for h in range(2):
            r = x * 16 + 8 * h
            rows, inner_rows, after = eight(r), eight(r + PAD), eight(r + 2 * PAD)

            def six(f, ref):
                return [ref(after), ref(rows)] + [near[f, n, rows, :] for n in range(4)]

            wet = conc[IONS, inner_rows, :]
            swept = conc[FIELDS, inner_rows, :]
            near_wet = six(IONS, lambda s: conc[IONS, s, :])
            near_swept = six(FIELDS, lambda s: conc[FIELDS, s, :])
            flow = drift = None
            weights = {1.0: [], 0.5: [], -0.5: []}
            for n in range(6):
                g = wet * near_wet[n]
                d = g * (swept - near_swept[n])
                half = 0.5 * d
                flow = g if flow is None else flow + g
                drift = d if drift is None else drift + d
                weights[1.0].append(g - d)
                weights[0.5].append(g - half)
                weights[-0.5].append(g + half)
            totals = {half: flow + half * drift for half in weights}
            ions = [conc[i, inner_rows, :] for i in range(IONS)]
            reaction = jnp.where(
                wet > 0.0, activity * (ions[2] - ions[0] * ions[1] * (1.0 / solubility)), 0.0
            )
            for i in range(IONS):
                half = 0.5 * valences[i]
                neighbours_of = six(i, lambda s, i=i: conc[i, s, :])
                outflow = ions[i] * totals[half]
                for n in range(6):
                    outflow = outflow - weights[half][n] * neighbours_of[n]
                value = ions[i] - rates[i] * outflow
                if reaction_signs[i] > 0:
                    value = value + reaction
                elif reaction_signs[i] < 0:
                    value = value - reaction
                updated[i, rows, :] = value
            relaxed[rows, :] = swept
        return carry

    lax.fori_loop(0, SIDE, finish, 0)


def close(number, *operands):
    f32 = jnp.float32
    padded = ROWS + 2 * PAD
    states = SWEEPS - FIRST + 1
    hbm = pl.BlockSpec(memory_space=pl.ANY)
    vmem = pl.BlockSpec(memory_space=pltpu.VMEM)
    smem = pl.BlockSpec(memory_space=pltpu.SMEM)
    new_species, new_potential = pl.pallas_call(
        partial(close_kernel, PAIRS[number]),
        out_shape=(
            jax.ShapeDtypeStruct((IONS, ROWS, 128), f32),
            jax.ShapeDtypeStruct((ROWS, 128), f32),
        ),
        in_specs=[hbm] * 5 + [smem] * 5,
        out_specs=(vmem, vmem),
        scratch_shapes=[
            pltpu.VMEM((2, padded, 128), f32),
            pltpu.VMEM((FIELDS + 1, padded, 128), f32),
            pltpu.VMEM((FIELDS + 1, 4, ROWS, 128), f32),
            pltpu.VMEM((ROWS, 128), f32),
            pltpu.VMEM((6, FIELDS + 1, 16, 128), f32),
            pltpu.VMEM((states, 4, 16, 128), f32),
            pltpu.VMEM((states, 6, 16, 128), f32),
            pltpu.VMEM((FIELDS + 1, SHARE, 128), f32),
            pltpu.VMEM((2, FIELDS + 1, SHARE, 128), f32),
            pltpu.SemaphoreType.DMA((5,)),
            pltpu.SemaphoreType.DMA((states, 6)),
            pltpu.SemaphoreType.DMA((states, 6)),
            pltpu.SemaphoreType.DMA((2, FIELDS + 2)),
            pltpu.SemaphoreType.DMA((2, FIELDS + 2)),
        ],
        compiler_params=pltpu.CompilerParams(
            collective_id=1 + number, has_side_effects=True, vmem_limit_bytes=40 * 1024 * 1024
        ),
        name=f"close_{number}",
    )(*operands)
    return as_bricks(new_species), as_bricks(new_potential)


def as_rows(field):
    lead = field.shape[:-2]
    split = field.reshape(lead + (2, ROWS // 2, 128))
    return jnp.swapaxes(split, -3, -2).reshape(lead + (ROWS, 128))


def as_bricks(rows):
    lead = rows.shape[:-2]
    split = rows.reshape(lead + (ROWS // 2, 2, 128))
    return jnp.swapaxes(split, -3, -2).reshape(lead + (2, ROWS // 2 * 128))


def local(
    species, potential, pore, openness, neighbours, diffusivity, rate_const, opened, partner, give_slot
):
    hbm = pl.BlockSpec(memory_space=pl.ANY)
    smem = pl.BlockSpec(memory_space=pltpu.SMEM)
    f32 = jnp.float32
    padded = ROWS + 2 * PAD
    *carried, choice, control = pl.pallas_call(
        open_kernel,
        out_shape=(
            jax.ShapeDtypeStruct((padded, 128), f32),
            jax.ShapeDtypeStruct((FIELDS, padded, 128), f32),
            jax.ShapeDtypeStruct((ROWS, 128), f32),
            jax.ShapeDtypeStruct((6, FIELDS, 16, 128), f32),
            jax.ShapeDtypeStruct((4, 16, 128), f32),
            jax.ShapeDtypeStruct((1,), jnp.int32),
            jax.ShapeDtypeStruct((3,), jnp.int32),
        ),
        in_specs=[hbm] * 4 + [smem] * 3,
        out_specs=(hbm,) * 5 + (smem, smem),
        scratch_shapes=[
            pltpu.VMEM((2, padded, 128), f32),
            pltpu.VMEM((FIELDS, padded, 128), f32),
            pltpu.VMEM((ROWS, 128), f32),
            pltpu.VMEM((ROWS, 128), jnp.int32),
            pltpu.VMEM((ROWS, 128), f32),
            pltpu.VMEM((FIRST + 1, 4, 16, 128), f32),
            pltpu.VMEM((FIRST, 6, 16, 128), f32),
            pltpu.VMEM((4, FIELDS, 16, 128), f32),
            pltpu.VMEM((6, FIELDS, 16, 128), f32),
            pltpu.VMEM((2, 8, 128), f32),
            pltpu.VMEM((2, 15, 8, 128), f32),
            pltpu.SemaphoreType.DMA((3 + IONS,)),
            pltpu.SemaphoreType.DMA((5,)),
            pltpu.SemaphoreType.DMA((FIRST, 6)),
            pltpu.SemaphoreType.DMA((FIRST, 6)),
            pltpu.SemaphoreType.DMA((6,)),
            pltpu.SemaphoreType.DMA((6,)),
            pltpu.SemaphoreType.DMA((2, 15)),
            pltpu.SemaphoreType.DMA((2, 15)),
        ],
        compiler_params=pltpu.CompilerParams(collective_id=0, has_side_effects=True),
        name="open",
    )(
        as_rows(potential),
        as_rows(pore),
        as_rows(openness),
        as_rows(species),
        neighbours,
        partner,
        give_slot,
    )
    new_species, new_potential = lax.switch(
        choice[0],
        [partial(close, number) for number in range(len(PAIRS))],
        *carried,
        neighbours,
        diffusivity,
        rate_const,
        opened,
        control,
    )
    return new_species, new_potential


def solution(mesh):
    in_specs = (
        P(None, ("group", "dev"), None),
        P(("group", "dev"), None),
        P(("group", "dev"), None),
        P(("group", "dev"), None),
        P(("group", "dev"), None),
        P(),
        P(("group", "dev")),
        P(("group", "dev")),
        P(("group", "dev")),
        P(("group", "dev")),
    )
    out_specs = (P(None, ("group", "dev"), None), P(("group", "dev"), None))
    return jax.shard_map(local, mesh=mesh, in_specs=in_specs, out_specs=out_specs, check_vma=False)
```
